32 devices in a mesh: tp: 4 (over y, core), grp: 8 (over z, x).
Axes of the slice: x: 2, y: 2, z: 4, core: 2. Of those that a mesh axis runs over, the one named last changes fastest.
Arguments:
- teacher_state: bfloat16 [2048, 5280], P('grp'), may hold values from -6 to 6
- injection: bfloat16 [2048, 5280], P('grp'), may hold values from -6 to 6
- teacher_up: bfloat16 [5280, 8960], P(None, 'tp'), may hold values from -0.078125 to 0.078125
- teacher_down: bfloat16 [8960, 5280], P('tp', 'grp'), may hold values from -0.0625 to 0.0625
- student_up: bfloat16 [5280, 256], P('grp', 'tp'), may hold values from -0.078125 to 0.078125
- student_down: bfloat16 [256, 5280], P('tp', 'grp'), may hold values from -0.375 to 0.375
- teacher_step: int32 [2], replicated, may hold values from 0 to 1
- student_depth: int32 [2], replicated, may hold values from 1 to 2
Outputs:
- grad_up: float32 [5280, 256], P('grp', 'tp')
- grad_down: float32 [256, 5280], P('tp', 'grp')
The draws below stay inside these ranges and needn't reach their ends.
All inputs are finite; a program needn't handle non-finite values.
Results may differ from the reference program's by a relative error of at most 0.02.
Values may be sent and summed in bfloat16 or wider, within the bound.
No kernel may reach another device: no remote copies, remote signals or barrier semaphores. Data moves between devices by JAX's collectives and lax.ppermute only.
A program may use at most 192 MiB of HBM per device.

```python
import jax
import jax.numpy as jnp
from jax import lax

D = 5280
SH = 256
TOK_G = 256
LENGTH = 1024
T_ITERS = 1
S_ITERS = 2
H_T = 8960
TOKENS = 2048
SEQS = 2
N_TP = 4
N_GRP = 8


def with_spikes(drawn, key, source, target, shards_of, factor):
    def block_of(axis_at):
        return (jnp.arange(drawn.shape[axis_at]) // (drawn.shape[axis_at] // shards_of)).reshape((-1,) + (1,) * (drawn.ndim - 1 - axis_at))

    near = jax.random.permutation(key, shards_of)[block_of(target)]
    second = (block_of(target) + shards_of // 2) % shards_of
    return jnp.where((block_of(source) == near) | (block_of(source) == second), factor * drawn, drawn)


def block_scale(rng, shape, shards, low, largest):
    def one(axis_at, shards_of):
        heights = jax.random.uniform(jax.random.fold_in(jax.random.fold_in(rng, 6), axis_at), (shards_of,), jnp.float32, low / len(shards), largest / len(shards))
        return jnp.repeat(jnp.exp(heights), shape[axis_at] // shards_of).reshape((-1,) + (1,) * (len(shape) - axis_at - 1))

    loudness = one(*shards[0])
    for cut in shards[1:]:
        loudness = loudness * one(*cut)
    return loudness


def normal_values(rng, shape, scale, most, split=(), kind=jnp.bfloat16):
    factor_of = block_scale(rng, shape, split, -0.22, 0.18) if split else 1.0
    array = jax.random.normal(rng, shape, jnp.float32) * scale * factor_of
    return jnp.minimum(jnp.maximum(array, -most), most).astype(kind)


def heavy_noise(stream_key, shape, scale, most, pieces, heavy, kind=jnp.bfloat16):
    entries = scale * jax.random.normal(stream_key, shape, jnp.float32)
    if pieces:
        entries = entries * block_scale(stream_key, shape, pieces, -0.22, 0.18)
    return jnp.clip(with_spikes(entries, jax.random.fold_in(stream_key, 3), *heavy), -most, most).astype(kind)


def setup_inputs(seed: int = 0) -> dict:
    seeds = jax.random.split(jax.random.key(seed), 9)
    return {
        "teacher_state": normal_values(seeds[0], (TOKENS, D), 1.0, 6.0, ((0, 8),)),
        "injection": heavy_noise(seeds[1], (TOKENS, D), 1.0, 6.0, ((0, 8),), (0, 1, 8, 2.0)),
        "teacher_up": normal_values(seeds[2], (D, H_T), D ** -0.5, 0.078125, ((1, 4),)),
        "teacher_down": normal_values(seeds[3], (H_T, D), H_T ** -0.5, 0.0625, ((0, 4), (1, 8))),
        "student_up": normal_values(seeds[4], (D, SH), D ** -0.5, 0.078125, ((0, 8), (1, 4))),
        "student_down": normal_values(seeds[5], (SH, D), SH ** -0.5, 0.375, ((0, 4), (1, 8))),
        "teacher_step": jax.random.randint(seeds[6], (SEQS,), 0, T_ITERS + 1).astype(jnp.int32),
        "student_depth": jax.random.randint(seeds[7], (SEQS,), 1, S_ITERS + 1).astype(jnp.int32),
    }


epsilon = 1e-06
loss_scale = 64.0

def normalize(summed):
    return lax.rsqrt(lax.optimization_barrier(jnp.mean(summed * summed, axis=-1, keepdims=True)) + epsilon)

def silu_slope(logits):
    sigmoid = jax.nn.sigmoid(logits)
    return sigmoid * (1.0 + logits * (1.0 - sigmoid))

def teacher_delta(normed, teacher_up, teacher_down):
    width = teacher_up.shape[1] // N_TP
    totals = jnp.zeros((normed.shape[0], teacher_down.shape[1]), jnp.float32)
    for member in range(N_TP):
        hidden = jax.nn.silu(jnp.dot(normed, teacher_up[:, member * width:(member + 1) * width], preferred_element_type=jnp.float32)).astype(jnp.bfloat16)
        partial_sum = jnp.dot(hidden, teacher_down[member * width:(member + 1) * width], preferred_element_type=jnp.float32).astype(jnp.bfloat16)
        partial_sum = lax.optimization_barrier(partial_sum)
        totals = totals + partial_sum.astype(jnp.float32)
    return totals

def teacher_block(state, injection, teacher_up, teacher_down):
    latents = []
    current = state
    for iteration in range(T_ITERS):
        summed = current.astype(jnp.float32) + injection.astype(jnp.float32)
        normed = (summed * normalize(summed)).astype(jnp.bfloat16)
        current = (current.astype(jnp.float32) + teacher_delta(normed, teacher_up, teacher_down)).astype(jnp.bfloat16)
        latents.append(current)
    return tuple(latents)

def student_grads(start, injection, latents, pick_teacher, pick_depth, student_up, student_down, row_count):
    previous = start
    records = []
    outputs = []
    for iteration in range(S_ITERS):
        summed = previous.astype(jnp.float32) + injection.astype(jnp.float32)
        factor = normalize(summed)
        normed = (summed * factor).astype(jnp.bfloat16)
        logits = jnp.dot(normed, student_up, preferred_element_type=jnp.float32)
        hidden = jax.nn.silu(logits).astype(jnp.bfloat16)
        previous = (previous.astype(jnp.float32) + jnp.dot(hidden, student_down, preferred_element_type=jnp.float32)).astype(jnp.bfloat16)
        records.append((summed, factor, normed, logits, hidden))
        outputs.append(previous)
    target = start.astype(jnp.float32)
    for iteration in range(len(latents)):
        target = jnp.where(pick_teacher[:, None] == iteration + 1, latents[iteration].astype(jnp.float32), target)
    result = jnp.zeros(start.shape, jnp.float32)
    for iteration in range(S_ITERS):
        result = jnp.where(pick_depth[:, None] == iteration + 1, outputs[iteration].astype(jnp.float32), result)
    slope = loss_scale * 2.0 / row_count * (result - target)
    grad_up = jnp.zeros(student_up.shape, jnp.float32)
    grad_down = jnp.zeros(student_down.shape, jnp.float32)
    carried = jnp.zeros(start.shape, jnp.float32)
    for iteration in reversed(range(S_ITERS)):
        summed, factor, normed, logits, hidden = records[iteration]
        cotangent = carried + jnp.where(pick_depth[:, None] == iteration + 1, slope, 0.0)
        rounded = cotangent.astype(jnp.bfloat16)
        grad_down = grad_down + jnp.dot(hidden.T, rounded, preferred_element_type=jnp.float32)
        upstream = jnp.dot(rounded, student_down.T, preferred_element_type=jnp.float32)
        local_grad = (upstream * silu_slope(logits)).astype(jnp.bfloat16)
        grad_up = grad_up + jnp.dot(normed.T, local_grad, preferred_element_type=jnp.float32)
        if iteration > 0:
            back_flow = jnp.dot(local_grad, student_up.T, preferred_element_type=jnp.float32)
            carried = cotangent + factor * back_flow - summed * factor ** 3 * lax.optimization_barrier(jnp.mean(summed * back_flow, axis=-1, keepdims=True))
    return (grad_up, grad_down)

def reference(teacher_state, injection, teacher_up, teacher_down, student_up, student_down, teacher_step, student_depth):
    blocks_state = teacher_state.reshape(N_GRP, TOK_G, D)
    blocks_inject = injection.reshape(N_GRP, TOK_G, D)

    def run_block(paired):
        return teacher_block(paired[0], paired[1], teacher_up, teacher_down)
    stacked = lax.map(run_block, (blocks_state, blocks_inject))
    latents = [member_latent.reshape(TOKENS, D) for member_latent in stacked]
    sequence = jnp.arange(TOKENS, dtype=jnp.int32) // LENGTH
    pick_teacher = teacher_step[sequence]
    pick_depth = student_depth[sequence]
    grad_up, grad_down = student_grads(teacher_state, injection, latents, pick_teacher, pick_depth, student_up, student_down, TOKENS)
    return (grad_up, grad_down)
```

```python
import jax
import jax.numpy as jnp
from jax import lax
from jax.sharding import PartitionSpec as P

LENGTH = 1024
PAIR = 2

epsilon = 1e-06
loss_scale = 64.0


f32, bf16 = jnp.float32, jnp.bfloat16


def dot(left, right, contract):
    return lax.dot_general(left, right, (contract, ((), ())), preferred_element_type=f32)


def silu_slope(logits):
    sigmoid = jax.nn.sigmoid(logits)
    return sigmoid * (1.0 + logits * (1.0 - sigmoid))


def pick(stacked, index):
    return lax.dynamic_index_in_dim(stacked, index, 0, keepdims=False)


def after(value, *earlier):
    return lax.optimization_barrier((value, *earlier))[0]


def swapped(first, second, flag):
    return jnp.where(flag, jnp.stack([second, first]), jnp.stack([first, second]))


def body(
    teacher_state,
    injection,
    teacher_up,
    teacher_down,
    student_up,
    student_down,
    teacher_step,
    student_depth,
):
    slices, groups = lax.axis_size("tp"), lax.axis_size("grp")
    line = groups // PAIR
    member, group = lax.axis_index("tp"), lax.axis_index("grp")
    spot, side = group // PAIR, group % PAIR
    core, row = member % 2, member // 2
    rows, width = teacher_state.shape
    half = rows // 2
    units, piece = student_down.shape
    block = PAIR * piece
    window = (piece + 7) // 8 * 8
    offset = block - window

    def swap_side(value):
        return lax.ppermute(value, "grp", [(g, g ^ 1) for g in range(groups)])

    def send(value, moves):
        pairs = [(a * PAIR + s, b * PAIR + s) for a, b in moves for s in range(PAIR)]
        return lax.ppermute(value, "grp", pairs)

    def along(value, hop):
        return send(value, [(z, z ^ hop) for z in range(line)])

    def swap_core(value):
        return lax.ppermute(value, "tp", [(t, t ^ 1) for t in range(slices)])

    def swap_y(value):
        return lax.ppermute(value, "tp", [(t, t ^ 2) for t in range(slices)])

    down_own = teacher_down.T
    down_other = swap_side(down_own)
    small = jnp.concatenate([student_up, student_down.T], axis=1)
    spare = window - piece
    small = jnp.where(
        side == 0,
        jnp.pad(small, ((0, spare), (0, 0))),
        jnp.pad(small, ((spare, 0), (0, 0))),
    )
    arrived = [along(small, hop) for hop in range(1, line)]

    state = teacher_state.T
    inject = injection.T
    summed = state.astype(f32) + inject.astype(f32)
    factor = lax.rsqrt(jnp.mean(summed * summed, axis=0, keepdims=True) + epsilon)
    normed = (summed * factor).astype(bf16)

    def expand(columns, value):
        return jax.nn.silu(dot(columns, value, ((0,), (0,)))).astype(bf16)

    if line == 4:
        share = width // slices
        quarter = lax.dynamic_slice_in_dim(normed, member * share, share, 0)
        far = send(quarter, [(0, 3), (3, 0)])
        own_block = expand(teacher_up, normed)
        middle = [(1, 2), (2, 1)]
        outward = [(1, 0), (2, 3)]
        inner = (spot == 1) | (spot == 2)
        near = along(own_block, 1)
        cross_own = send(own_block, middle)
        far = swapped(far, swap_y(far), row == 1)
        far = swapped(far, swap_core(far), core == 1).swapaxes(0, 1)
        far = lax.optimization_barrier(far.reshape(width, rows))
        far_block = expand(teacher_up, far)
        out_own = send(cross_own, outward)
        cross_next = send(near, middle)
        blocks = [
            own_block,
            near,
            jnp.where(inner, cross_next, out_own),
            jnp.where(inner, cross_own, far_block),
        ]
    else:
        own_block = expand(teacher_up, normed)
        blocks = [own_block] + [along(own_block, hop) for hop in range(1, line)]

    arrived = jnp.stack([small] + arrived)
    arrived = jnp.stack([pick(arrived, spot ^ z) for z in range(line)])
    arrived = after(arrived, own_block)
    other = swap_y(arrived)
    parts = lax.optimization_barrier(
        (
            jnp.concatenate([arrived[:, :, :units], other[:, :, :units]], axis=2),
            jnp.concatenate([arrived[:, :, units:], other[:, :, units:]], axis=2),
        )
    )

    def all_units(part):
        other = swap_side(part)
        first = jnp.where(side == 0, part, other)
        second = jnp.where(side == 0, other, part)
        tail, head = ((0, 0), (0, offset), (0, 0)), ((0, 0), (offset, 0), (0, 0))
        part = (jnp.pad(first, tail) + jnp.pad(second, head)).reshape(width, 2 * units)
        other = swap_core(part)
        return lax.optimization_barrier(jnp.concatenate([part, other], axis=1))

    up_all, down_all = all_units(parts[0]), all_units(parts[1])

    def tile(value):
        own = dot(down_own, value, ((1,), (0,))).astype(bf16)
        other = dot(down_other, value, ((1,), (0,))).astype(bf16)
        own, other = lax.optimization_barrier((own, other))
        whole = jnp.where(
            side == 0,
            jnp.concatenate([own, other], axis=0),
            jnp.concatenate([other, own], axis=0),
        )
        low, high = whole[:, :half], whole[:, half:]
        return jnp.where(core == 0, low, high), jnp.where(core == 0, high, low)

    def rows_of(value, index):
        return lax.dynamic_slice_in_dim(value, index * offset, window, value.ndim - 2)

    deltas = [None] * line
    order = [0, 1, 3, 2] if line == 4 else list(range(line))
    for hop in order:
        kept, given = tile(blocks[hop])
        other = swap_core(given)
        chip = (kept.astype(f32) + other.astype(f32)).astype(bf16)
        other = swap_y(rows_of(chip, 1 - row))
        part = (rows_of(chip, row).astype(f32) + other.astype(f32)).astype(bf16)
        if hop:
            part = along(part, hop)
        other = swap_y(part)
        features = jnp.where(
            row == 0,
            jnp.concatenate([part, other[2 * window - block :]], axis=0),
            jnp.concatenate([other, part[2 * window - block :]], axis=0),
        )
        other = swap_core(features)
        deltas[hop] = jnp.where(
            core == 0,
            jnp.concatenate([features, other], axis=1),
            jnp.concatenate([other, features], axis=1),
        )
    deltas = jnp.stack(deltas)
    delta = jnp.stack([pick(deltas, spot ^ z) for z in range(line)])
    delta = delta.reshape(width, rows)

    normed1 = normed
    logits1 = dot(up_all, normed1, ((0,), (0,)))
    hidden1 = jax.nn.silu(logits1).astype(bf16)
    state1 = (state.astype(f32) + dot(down_all, hidden1, ((1,), (0,)))).astype(bf16)
    summed2 = state1.astype(f32) + inject.astype(f32)
    factor2 = lax.rsqrt(jnp.sum(summed2 * summed2, axis=0, keepdims=True) / width + epsilon)
    normed2 = (summed2 * factor2).astype(bf16)
    logits2 = dot(up_all, normed2, ((0,), (0,)))
    hidden2 = jax.nn.silu(logits2).astype(bf16)
    state2 = (state1.astype(f32) + dot(down_all, hidden2, ((1,), (0,)))).astype(bf16)

    sequence = (group * rows + jnp.arange(rows, dtype=jnp.int32)) // LENGTH
    steps = jnp.arange(teacher_step.shape[0], dtype=jnp.int32)[:, None]
    matches = sequence[None, :] == steps
    pick_teacher = jnp.sum(jnp.where(matches, teacher_step[:, None], 0), axis=0)[None, :]
    pick_depth = jnp.sum(jnp.where(matches, student_depth[:, None], 0), axis=0)[None, :]
    result = jnp.where(pick_depth == 1, state1, state2)
    result, state, summed2, factor2, normed2, logits1, logits2, hidden1, hidden2 = (
        lax.optimization_barrier(
            (result, state, summed2, factor2, normed2, logits1, logits2, hidden1, hidden2)
        )
    )

    def own_units(value):
        return value[:units]

    def paired(grad):
        grad = grad.astype(bf16).reshape(line, block, units)
        kept, given = rows_of(grad, side), rows_of(grad, 1 - side)
        return (kept.astype(f32) + swap_side(given).astype(f32)).astype(bf16)

    def lined(value):
        total = pick(value, spot).astype(f32)
        for hop in range(1, line):
            moved = along(pick(value, spot ^ hop), hop)
            total = total + moved.astype(f32)
        return lax.dynamic_slice_in_dim(total, side * (window - piece), piece, 0)

    latent = (state.astype(f32) + delta.astype(f32)).astype(bf16)
    target = jnp.where(pick_teacher == 1, latent, state).astype(f32)
    slope = loss_scale * 2.0 / (rows * groups) * (result.astype(f32) - target)
    cotangent2 = jnp.where(pick_depth == 2, slope, 0.0)
    rounded2 = cotangent2.astype(bf16)
    upstream2 = dot(down_all, rounded2, ((0,), (0,)))
    local2 = (upstream2 * silu_slope(logits2)).astype(bf16)
    back_flow = dot(up_all, local2, ((1,), (0,)))
    mean_flow = jnp.sum(summed2 * back_flow, axis=0, keepdims=True) / width
    cotangent1 = (
        cotangent2
        + factor2 * back_flow
        - summed2 * factor2**3 * mean_flow
        + jnp.where(pick_depth == 1, slope, 0.0)
    )
    rounded1 = cotangent1.astype(bf16)
    grad_down = dot(rounded2, own_units(hidden2), ((1,), (1,))) + dot(
        rounded1, own_units(hidden1), ((1,), (1,))
    )
    grad_down = paired(grad_down)
    upstream1 = dot(down_all, rounded1, ((0,), (0,)))
    local1 = (upstream1 * silu_slope(logits1)).astype(bf16)
    grad_up = dot(normed2, own_units(local2), ((1,), (1,))) + dot(
        normed1, own_units(local1), ((1,), (1,))
    )
    grad_up = paired(grad_up)
    grads = lined(jnp.concatenate([grad_up, grad_down], axis=2))
    return grads[:, :units], grads[:, units:].T


def solution(mesh):
    in_specs = (
        P("grp", None),
        P("grp", None),
        P(None, "tp"),
        P("tp", "grp"),
        P("grp", "tp"),
        P("tp", "grp"),
        P(),
        P(),
    )
    out_specs = (P("grp", "tp"), P("tp", "grp"))

    return jax.shard_map(body, mesh=mesh, in_specs=in_specs, out_specs=out_specs, check_vma=False)
```

```python
import jax
import jax.numpy as jnp
from jax import lax
from jax.experimental import pallas as pl
from jax.experimental.pallas import tpu as pltpu
from jax.sharding import PartitionSpec as P

LENGTH = 1024
PAIR = 2

epsilon = 1e-06
loss_scale = 64.0


f32, bf16 = jnp.float32, jnp.bfloat16


def dot(left, right, contract):
    return lax.dot_general(left, right, (contract, ((), ())), preferred_element_type=f32)


def silu_slope(logits):
    sigmoid = jax.nn.sigmoid(logits)
    return sigmoid * (1.0 + logits * (1.0 - sigmoid))


def pick(stacked, index):
    return lax.dynamic_index_in_dim(stacked, index, 0, keepdims=False)


def after(value, *earlier):
    return lax.optimization_barrier((value, *earlier))[0]


def expand(weights, value):
    units, width = weights.shape
    steps = max(n for n in (4, 2, 1) if units % (16 * n) == 0 or n == 1)

    def kernel(weights_ref, value_ref, out_ref):
        out_ref[...] = jax.nn.silu(dot(weights_ref[...], value_ref[...], ((1,), (0,)))).astype(bf16)

    return pl.pallas_call(
        kernel,
        out_shape=jax.ShapeDtypeStruct((units, value.shape[1]), bf16),
        grid=(steps,),
        in_specs=[
            pl.BlockSpec((units // steps, width), lambda i: (i, 0)),
            pl.BlockSpec(value.shape, lambda i: (0, 0), pipeline_mode=pl.Buffered(1)),
        ],
        out_specs=pl.BlockSpec((units // steps, value.shape[1]), lambda i: (i, 0)),
        compiler_params=pltpu.CompilerParams(
            vmem_limit_bytes=(4 * units * width // steps + 2 * value.size) * 5 // 4 + 2**21
        ),
        cost_estimate=pl.CostEstimate(
            flops=2 * units * width * value.shape[1],
            transcendentals=units * value.shape[1],
            bytes_accessed=2 * (units * width + (units + width) * value.shape[1]),
        ),
    )(weights, value)


def window_grads(late, early, units, side, line, block, window):
    offset = block - window
    own = units.shape[0] // 2

    def kernel(side_ref, late_ref, early_ref, units_ref, kept_ref, given_ref, theirs_ref):
        first = side_ref[0] == 0
        for z in range(line):
            halves = []
            for start in (z * block, z * block + offset):
                rows = pl.ds(start, window)
                features = jnp.concatenate([late_ref[rows, :], early_ref[rows, :]], axis=1)
                halves.append(dot(units_ref[...], features, ((1,), (1,))))
            low, high = halves
            kept, given = jnp.where(first, low, high), jnp.where(first, high, low)
            kept_ref[z] = kept[:own]
            given_ref[z] = given[:own]
            theirs_ref[0, z] = kept[own:].astype(bf16)
            theirs_ref[1, z] = given[own:].astype(bf16)

    shape = (line, own, window)
    vmem = pl.BlockSpec(memory_space=pltpu.VMEM)
    return pl.pallas_call(
        kernel,
        out_shape=(
            jax.ShapeDtypeStruct(shape, f32),
            jax.ShapeDtypeStruct(shape, f32),
            jax.ShapeDtypeStruct((2, *shape), bf16),
        ),
        in_specs=[pl.BlockSpec(memory_space=pltpu.SMEM), vmem, vmem, vmem],
        out_specs=(vmem, vmem, vmem),
        compiler_params=pltpu.CompilerParams(vmem_limit_bytes=8 * late.size + 2**23),
    )(side.reshape(1), late, early, units)


def body(
    teacher_state,
    injection,
    teacher_up,
    teacher_down,
    student_up,
    student_down,
    teacher_step,
    student_depth,
):
    slices, groups = lax.axis_size("tp"), lax.axis_size("grp")
    line = groups // PAIR
    member, group = lax.axis_index("tp"), lax.axis_index("grp")
    spot, side = group // PAIR, group % PAIR
    core, row = member % 2, member // 2
    rows, width = teacher_state.shape
    half = rows // 2
    units, piece = student_down.shape
    block = PAIR * piece
    window = (piece + 7) // 8 * 8
    offset = block - window

    def swap_side(value):
        return lax.ppermute(value, "grp", [(g, g ^ 1) for g in range(groups)])

    def send(value, moves):
        pairs = [(a * PAIR + s, b * PAIR + s) for a, b in moves for s in range(PAIR)]
        return lax.ppermute(value, "grp", pairs)

    def along(value, hop):
        return send(value, [(z, z ^ hop) for z in range(line)])

    def swap_core(value):
        return lax.ppermute(value, "tp", [(t, t ^ 1) for t in range(slices)])

    def swap_y(value):
        return lax.ppermute(value, "tp", [(t, t ^ 2) for t in range(slices)])

    down_own = teacher_down.T
    down_other = swap_side(down_own)
    small = jnp.concatenate([student_up, student_down.T], axis=1)
    spare = window - piece
    small = jnp.where(
        side == 0,
        jnp.pad(small, ((0, spare), (0, 0))),
        jnp.pad(small, ((spare, 0), (0, 0))),
    )
    arrived = [along(small, hop) for hop in range(1, line)]

    state = teacher_state.T
    inject = injection.T
    summed = state.astype(f32) + inject.astype(f32)
    factor = lax.rsqrt(jnp.mean(summed * summed, axis=0, keepdims=True) + epsilon)
    normed = (summed * factor).astype(bf16)

    up_own = teacher_up.T
    if line == 4:
        share = width // slices
        quarter = lax.dynamic_slice_in_dim(normed, member * share, share, 0)
        far = send(quarter, [(0, 3), (3, 0)])
        own_block = expand(up_own, normed)
        middle = [(1, 2), (2, 1)]
        outward = [(1, 0), (2, 3)]
        inner = (spot == 1) | (spot == 2)
        near = along(own_block, 1)
        cross_own = send(own_block, middle)
        other = swap_y(far)
        far = jnp.stack([far, swap_core(far), other, swap_core(other)])
        far = jnp.concatenate([pick(far, member ^ t) for t in range(slices)], axis=0)
        far = lax.optimization_barrier(far)
        far_block = expand(up_own, far)
        out_own = send(cross_own, outward)
        cross_next = send(near, middle)
        blocks = [
            own_block,
            near,
            jnp.where(inner, cross_next, out_own),
            jnp.where(inner, cross_own, far_block),
        ]
    else:
        own_block = expand(up_own, normed)
        blocks = [own_block] + [along(own_block, hop) for hop in range(1, line)]

    arrived = jnp.stack([small] + arrived)
    arrived = jnp.stack([pick(arrived, spot ^ z) for z in range(line)])
    arrived = after(arrived, own_block)
    other = swap_y(arrived)
    parts = jnp.stack(
        [
            jnp.concatenate([arrived[:, :, :units], other[:, :, :units]], axis=2),
            jnp.concatenate([arrived[:, :, units:], other[:, :, units:]], axis=2),
        ]
    )
    other = swap_side(parts)
    first, second = jnp.where(side == 0, parts, other), jnp.where(side == 0, other, parts)
    tail = ((0, 0), (0, 0), (0, offset), (0, 0))
    head = ((0, 0), (0, 0), (offset, 0), (0, 0))
    parts = (jnp.pad(first, tail) + jnp.pad(second, head)).reshape(2, width, 2 * units)
    other = swap_core(parts)
    up_all, down_all = lax.optimization_barrier(
        tuple(jnp.concatenate([parts[i], other[i]], axis=1) for i in range(2))
    )

    def tile(value):
        own = dot(down_own, value, ((1,), (0,))).astype(bf16)
        other = dot(down_other, value, ((1,), (0,))).astype(bf16)
        own, other = lax.optimization_barrier((own, other))
        whole = jnp.where(
            side == 0,
            jnp.concatenate([own, other], axis=0),
            jnp.concatenate([other, own], axis=0),
        )
        low, high = whole[:, :half], whole[:, half:]
        return jnp.where(core == 0, low, high), jnp.where(core == 0, high, low)

    def rows_of(value, index):
        return lax.dynamic_slice_in_dim(value, index * offset, window, value.ndim - 2)

    deltas = [None] * line
    order = [[0, 1], [3], [2]] if line == 4 else [[hop] for hop in range(line)]
    for hops in order:
        tiles = [tile(blocks[hop]) for hop in hops]
        kept, given = jnp.stack([t[0] for t in tiles]), jnp.stack([t[1] for t in tiles])
        other = swap_core(given)
        chip = (kept.astype(f32) + other.astype(f32)).astype(bf16)
        other = swap_y(rows_of(chip, 1 - row))
        part = (rows_of(chip, row).astype(f32) + other.astype(f32)).astype(bf16)
        pieces = [part[i] for i in range(len(hops))]
        part = jnp.stack([along(piece, hop) if hop else piece for piece, hop in zip(pieces, hops)])
        other = swap_y(part)
        features = jnp.where(
            row == 0,
            jnp.concatenate([part, other[:, 2 * window - block :]], axis=1),
            jnp.concatenate([other, part[:, 2 * window - block :]], axis=1),
        )
        for i, hop in enumerate(hops):
            deltas[hop] = features[i]
    deltas = jnp.stack(deltas)
    delta = jnp.stack([pick(deltas, spot ^ z) for z in range(line)])
    delta = delta.reshape(width, half)

    whole = lax.optimization_barrier((state, inject, normed, own_block))[:3]
    state, inject, normed1 = lax.optimization_barrier(
        tuple(jnp.where(core == 0, value[:, :half], value[:, half:]) for value in whole)
    )
    logits1 = dot(up_all, normed1, ((0,), (0,)))
    hidden1 = jax.nn.silu(logits1).astype(bf16)
    state1 = (state.astype(f32) + dot(down_all, hidden1, ((1,), (0,)))).astype(bf16)
    summed2 = state1.astype(f32) + inject.astype(f32)
    factor2 = lax.rsqrt(jnp.sum(summed2 * summed2, axis=0, keepdims=True) / width + epsilon)
    normed2 = (summed2 * factor2).astype(bf16)
    logits2 = dot(up_all, normed2, ((0,), (0,)))
    hidden2 = jax.nn.silu(logits2).astype(bf16)
    state2 = (state1.astype(f32) + dot(down_all, hidden2, ((1,), (0,)))).astype(bf16)

    first = group * rows + core * half
    sequence = (first + jnp.arange(half, dtype=jnp.int32)) // LENGTH
    steps = jnp.arange(teacher_step.shape[0], dtype=jnp.int32)[:, None]
    matches = sequence[None, :] == steps
    pick_teacher = jnp.sum(jnp.where(matches, teacher_step[:, None], 0), axis=0)[None, :]
    pick_depth = jnp.sum(jnp.where(matches, student_depth[:, None], 0), axis=0)[None, :]
    result = jnp.where(pick_depth == 1, state1, state2)
    result, state, summed2, factor2, normed2, logits1, logits2, hidden1, hidden2 = (
        lax.optimization_barrier(
            (result, state, summed2, factor2, normed2, logits1, logits2, hidden1, hidden2)
        )
    )

    def chip_units(value):
        return jnp.concatenate([value[:units], value[2 * units : 3 * units]], axis=0)

    def paired(late, early, units_late, units_early):
        joined = jnp.concatenate([chip_units(units_late), chip_units(units_early)], axis=1)
        kept, given, theirs = window_grads(late, early, joined, side, line, block, window)
        theirs = swap_core(theirs).astype(f32)
        other = swap_side((given + theirs[1]).astype(bf16))
        return (kept + theirs[0] + other.astype(f32)).astype(bf16)

    def lined(value):
        total = pick(value, spot).astype(f32)
        for hop in range(1, line):
            moved = along(pick(value, spot ^ hop), hop)
            total = total + moved.astype(f32)
        return jnp.where(side == 0, total[:, :piece], total[:, window - piece :])

    latent = (state.astype(f32) + delta.astype(f32)).astype(bf16)
    target = jnp.where(pick_teacher == 1, latent, state).astype(f32)
    slope = loss_scale * 2.0 / (rows * groups) * (result.astype(f32) - target)
    cotangent2 = jnp.where(pick_depth == 2, slope, 0.0)
    rounded2 = cotangent2.astype(bf16)
    upstream2 = dot(down_all, rounded2, ((0,), (0,)))
    local2 = (upstream2 * silu_slope(logits2)).astype(bf16)
    back_flow = dot(up_all, local2, ((1,), (0,)))
    mean_flow = jnp.sum(summed2 * back_flow, axis=0, keepdims=True) / width
    cotangent1 = (
        cotangent2
        + factor2 * back_flow
        - summed2 * factor2**3 * mean_flow
        + jnp.where(pick_depth == 1, slope, 0.0)
    )
    rounded1 = cotangent1.astype(bf16)
    grad_down = paired(rounded2, rounded1, hidden2, hidden1)
    upstream1 = dot(down_all, rounded1, ((0,), (0,)))
    local1 = (upstream1 * silu_slope(logits1)).astype(bf16)
    grad_up = paired(normed2, normed1, local2, local1)
    return lined(grad_up).T, lined(grad_down)


def solution(mesh):
    in_specs = (
        P("grp", None),
        P("grp", None),
        P(None, "tp"),
        P("tp", "grp"),
        P("grp", "tp"),
        P("tp", "grp"),
        P(),
        P(),
    )
    out_specs = (P("grp", "tp"), P("tp", "grp"))

    return jax.shard_map(body, mesh=mesh, in_specs=in_specs, out_specs=out_specs, check_vma=False)
```

```python
import jax
import jax.numpy as jnp
from jax import lax
from jax.experimental import pallas as pl
from jax.experimental.pallas import tpu as pltpu
from jax.sharding import PartitionSpec as P

LENGTH = 1024
PAIR = 2

epsilon = 1e-06
loss_scale = 64.0


f32, bf16 = jnp.float32, jnp.bfloat16


def dot(left, right, contract):
    return lax.dot_general(left, right, (contract, ((), ())), preferred_element_type=f32)


def silu_slope(logits):
    sigmoid = jax.nn.sigmoid(logits)
    return sigmoid * (1.0 + logits * (1.0 - sigmoid))


def pick(stacked, index):
    return lax.dynamic_index_in_dim(stacked, index, 0, keepdims=False)


def after(value, *earlier):
    return lax.optimization_barrier((value, *earlier))[0]


def expand(weights, value):
    units, width = weights.shape
    steps = max(n for n in (4, 2, 1) if units % (16 * n) == 0 or n == 1)
    size = units // steps

    def kernel(weights_ref, value_ref, out_ref, held, done):
        def fetch(i):
            at = pl.ds(pl.multiple_of(i * size, size), size)
            return at, pltpu.make_async_copy(weights_ref.at[at], held.at[at], done.at[i])

        for i in range(steps):
            fetch(i)[1].start()

        def step(i, carry):
            at, copy = fetch(i)
            copy.wait()
            out_ref[at, :] = jax.nn.silu(dot(held[at, :], value_ref[...], ((1,), (0,)))).astype(bf16)
            return carry

        lax.fori_loop(0, steps, step, 0)

    vmem = pl.BlockSpec(memory_space=pltpu.VMEM)
    return pl.pallas_call(
        kernel,
        out_shape=jax.ShapeDtypeStruct((units, value.shape[1]), bf16),
        in_specs=[pl.BlockSpec(memory_space=pl.ANY), vmem],
        out_specs=vmem,
        scratch_shapes=[pltpu.VMEM((units, width), bf16), pltpu.SemaphoreType.DMA((steps,))],
        compiler_params=pltpu.CompilerParams(vmem_limit_bytes=2 * units * width + 20 * 2**20),
        cost_estimate=pl.CostEstimate(
            flops=2 * units * width * value.shape[1],
            transcendentals=units * value.shape[1],
            bytes_accessed=2 * (units * width + (units + width) * value.shape[1]),
        ),
    )(weights, value)


def window_grads(late, early, units, side, line, block, window):
    offset = block - window
    own = units.shape[0] // 2

    def kernel(side_ref, late_ref, early_ref, units_ref, kept_ref, given_ref, theirs_ref):
        first = side_ref[0] == 0
        for z in range(line):
            halves = []
            for start in (z * block, z * block + offset):
                rows = pl.ds(start, window)
                features = jnp.concatenate([late_ref[rows, :], early_ref[rows, :]], axis=1)
                halves.append(dot(units_ref[...], features, ((1,), (1,))))
            low, high = halves
            kept, given = jnp.where(first, low, high), jnp.where(first, high, low)
            kept_ref[z] = kept[:own]
            given_ref[z] = given[:own]
            theirs_ref[0, z] = kept[own:].astype(bf16)
            theirs_ref[1, z] = given[own:].astype(bf16)

    shape = (line, own, window)
    vmem = pl.BlockSpec(memory_space=pltpu.VMEM)
    return pl.pallas_call(
        kernel,
        out_shape=(
            jax.ShapeDtypeStruct(shape, f32),
            jax.ShapeDtypeStruct(shape, f32),
            jax.ShapeDtypeStruct((2, *shape), bf16),
        ),
        in_specs=[pl.BlockSpec(memory_space=pltpu.SMEM), vmem, vmem, vmem],
        out_specs=(vmem, vmem, vmem),
        compiler_params=pltpu.CompilerParams(vmem_limit_bytes=8 * late.size + 2**23),
    )(side.reshape(1), late, early, units)


def body(
    teacher_state,
    injection,
    teacher_up,
    teacher_down,
    student_up,
    student_down,
    teacher_step,
    student_depth,
):
    slices, groups = lax.axis_size("tp"), lax.axis_size("grp")
    line = groups // PAIR
    member, group = lax.axis_index("tp"), lax.axis_index("grp")
    spot, side = group // PAIR, group % PAIR
    core, row = member % 2, member // 2
    rows, width = teacher_state.shape
    half = rows // 2
    units, piece = student_down.shape
    block = PAIR * piece
    window = (piece + 7) // 8 * 8
    offset = block - window

    def swap_side(value):
        return lax.ppermute(value, "grp", [(g, g ^ 1) for g in range(groups)])

    def send(value, moves):
        pairs = [(a * PAIR + s, b * PAIR + s) for a, b in moves for s in range(PAIR)]
        return lax.ppermute(value, "grp", pairs)

    def along(value, hop):
        return send(value, [(z, z ^ hop) for z in range(line)])

    def swap_core(value):
        return lax.ppermute(value, "tp", [(t, t ^ 1) for t in range(slices)])

    def swap_y(value):
        return lax.ppermute(value, "tp", [(t, t ^ 2) for t in range(slices)])

    down_own = teacher_down.T
    down_other = swap_side(down_own)
    small = jnp.concatenate([student_up, student_down.T], axis=1)
    spare = window - piece
    small = jnp.where(
        side == 0,
        jnp.pad(small, ((0, spare), (0, 0))),
        jnp.pad(small, ((spare, 0), (0, 0))),
    )
    arrived = [along(small, hop) for hop in range(1, line)]

    state = teacher_state.T
    inject = injection.T
    summed = state.astype(f32) + inject.astype(f32)
    factor = lax.rsqrt(jnp.mean(summed * summed, axis=0, keepdims=True) + epsilon)
    normed = (summed * factor).astype(bf16)

    up_own = teacher_up.T
    if line == 4:
        share = width // slices
        quarter = lax.dynamic_slice_in_dim(normed, member * share, share, 0)
        far = send(quarter, [(0, 3), (3, 0)])
        own_block = expand(up_own, normed)
        middle = [(1, 2), (2, 1)]
        outward = [(1, 0), (2, 3)]
        inner = (spot == 1) | (spot == 2)
        near = along(own_block, 1)
        cross_own = send(own_block, middle)
        other = swap_y(far)
        far = jnp.stack([far, swap_core(far), other, swap_core(other)])
        far = jnp.concatenate([pick(far, member ^ t) for t in range(slices)], axis=0)
        far = lax.optimization_barrier(far)
        far_block = expand(up_own, far)
        out_own = send(cross_own, outward)
        cross_next = send(near, middle)
        blocks = [
            own_block,
            near,
            jnp.where(inner, cross_next, out_own),
            jnp.where(inner, cross_own, far_block),
        ]
    else:
        own_block = expand(up_own, normed)
        blocks = [own_block] + [along(own_block, hop) for hop in range(1, line)]

    arrived = jnp.stack([small] + arrived)
    arrived = jnp.stack([pick(arrived, spot ^ z) for z in range(line)])
    arrived = after(arrived, own_block)
    other = swap_y(arrived)
    parts = jnp.stack(
        [
            jnp.concatenate([arrived[:, :, :units], other[:, :, :units]], axis=2),
            jnp.concatenate([arrived[:, :, units:], other[:, :, units:]], axis=2),
        ]
    )
    other = swap_side(parts)
    first, second = jnp.where(side == 0, parts, other), jnp.where(side == 0, other, parts)
    tail = ((0, 0), (0, 0), (0, offset), (0, 0))
    head = ((0, 0), (0, 0), (offset, 0), (0, 0))
    parts = (jnp.pad(first, tail) + jnp.pad(second, head)).reshape(2, width, 2 * units)
    other = swap_core(parts)
    up_all, down_all = lax.optimization_barrier(
        tuple(jnp.concatenate([parts[i], other[i]], axis=1) for i in range(2))
    )

    def tile(value):
        own = dot(down_own, value, ((1,), (0,))).astype(bf16)
        other = dot(down_other, value, ((1,), (0,))).astype(bf16)
        own, other = lax.optimization_barrier((own, other))
        whole = jnp.where(
            side == 0,
            jnp.concatenate([own, other], axis=0),
            jnp.concatenate([other, own], axis=0),
        )
        low, high = whole[:, :half], whole[:, half:]
        return jnp.where(core == 0, low, high), jnp.where(core == 0, high, low)

    def rows_of(value, index):
        return lax.dynamic_slice_in_dim(value, index * offset, window, value.ndim - 2)

    deltas = [None] * line
    order = [[0, 1], [3], [2]] if line == 4 else [[hop] for hop in range(line)]
    for hops in order:
        tiles = [tile(blocks[hop]) for hop in hops]
        kept, given = jnp.stack([t[0] for t in tiles]), jnp.stack([t[1] for t in tiles])
        other = swap_core(given)
        chip = (kept.astype(f32) + other.astype(f32)).astype(bf16)
        other = swap_y(rows_of(chip, 1 - row))
        part = (rows_of(chip, row).astype(f32) + other.astype(f32)).astype(bf16)
        pieces = [part[i] for i in range(len(hops))]
        part = jnp.stack([along(piece, hop) if hop else piece for piece, hop in zip(pieces, hops)])
        other = swap_y(part)
        features = jnp.where(
            row == 0,
            jnp.concatenate([part, other[:, 2 * window - block :]], axis=1),
            jnp.concatenate([other, part[:, 2 * window - block :]], axis=1),
        )
        for i, hop in enumerate(hops):
            deltas[hop] = features[i]
    deltas = jnp.stack(deltas)
    delta = jnp.stack([pick(deltas, spot ^ z) for z in range(line)])
    delta = delta.reshape(width, half)

    whole = lax.optimization_barrier((state, inject, normed, own_block))[:3]
    state, inject, normed1 = lax.optimization_barrier(
        tuple(jnp.where(core == 0, value[:, :half], value[:, half:]) for value in whole)
    )
    logits1 = dot(up_all, normed1, ((0,), (0,)))
    hidden1 = jax.nn.silu(logits1).astype(bf16)
    state1 = (state.astype(f32) + dot(down_all, hidden1, ((1,), (0,)))).astype(bf16)
    summed2 = state1.astype(f32) + inject.astype(f32)
    factor2 = lax.rsqrt(jnp.sum(summed2 * summed2, axis=0, keepdims=True) / width + epsilon)
    normed2 = (summed2 * factor2).astype(bf16)
    logits2 = dot(up_all, normed2, ((0,), (0,)))
    hidden2 = jax.nn.silu(logits2).astype(bf16)
    state2 = (state1.astype(f32) + dot(down_all, hidden2, ((1,), (0,)))).astype(bf16)

    first = group * rows + core * half
    sequence = (first + jnp.arange(half, dtype=jnp.int32)) // LENGTH
    steps = jnp.arange(teacher_step.shape[0], dtype=jnp.int32)[:, None]
    matches = sequence[None, :] == steps
    pick_teacher = jnp.sum(jnp.where(matches, teacher_step[:, None], 0), axis=0)[None, :]
    pick_depth = jnp.sum(jnp.where(matches, student_depth[:, None], 0), axis=0)[None, :]
    result = jnp.where(pick_depth == 1, state1, state2)
    result, state, summed2, factor2, normed2, logits1, logits2, hidden1, hidden2 = (
        lax.optimization_barrier(
            (result, state, summed2, factor2, normed2, logits1, logits2, hidden1, hidden2)
        )
    )

    def chip_units(value):
        return jnp.concatenate([value[:units], value[2 * units : 3 * units]], axis=0)

    def paired(late, early, units_late, units_early):
        joined = jnp.concatenate([chip_units(units_late), chip_units(units_early)], axis=1)
        kept, given, theirs = window_grads(late, early, joined, side, line, block, window)
        theirs = swap_core(theirs).astype(f32)
        other = swap_side((given + theirs[1]).astype(bf16))
        return (kept + theirs[0] + other.astype(f32)).astype(bf16)

    def lined(value):
        total = pick(value, spot).astype(f32)
        for hop in range(1, line):
            moved = along(pick(value, spot ^ hop), hop)
            total = total + moved.astype(f32)
        return jnp.where(side == 0, total[:, :piece], total[:, window - piece :])

    latent = (state.astype(f32) + delta.astype(f32)).astype(bf16)
    target = jnp.where(pick_teacher == 1, latent, state).astype(f32)
    slope = loss_scale * 2.0 / (rows * groups) * (result.astype(f32) - target)
    cotangent2 = jnp.where(pick_depth == 2, slope, 0.0)
    rounded2 = cotangent2.astype(bf16)
    upstream2 = dot(down_all, rounded2, ((0,), (0,)))
    local2 = (upstream2 * silu_slope(logits2)).astype(bf16)
    back_flow = dot(up_all, local2, ((1,), (0,)))
    mean_flow = jnp.sum(summed2 * back_flow, axis=0, keepdims=True) / width
    cotangent1 = (
        cotangent2
        + factor2 * back_flow
        - summed2 * factor2**3 * mean_flow
        + jnp.where(pick_depth == 1, slope, 0.0)
    )
    rounded1 = cotangent1.astype(bf16)
    grad_down = paired(rounded2, rounded1, hidden2, hidden1)
    upstream1 = dot(down_all, rounded1, ((0,), (0,)))
    local1 = (upstream1 * silu_slope(logits1)).astype(bf16)
    grad_up = paired(normed2, normed1, local2, local1)
    return lined(grad_up).T, lined(grad_down)


def solution(mesh):
    in_specs = (
        P("grp", None),
        P("grp", None),
        P(None, "tp"),
        P("tp", "grp"),
        P("grp", "tp"),
        P("tp", "grp"),
        P(),
        P(),
    )
    out_specs = (P("grp", "tp"), P("tp", "grp"))

    return jax.shard_map(body, mesh=mesh, in_specs=in_specs, out_specs=out_specs, check_vma=False)
```

```python
import jax
import jax.numpy as jnp
from jax import lax
from jax.experimental import pallas as pl
from jax.experimental.pallas import tpu as pltpu
from jax.sharding import PartitionSpec as P

LENGTH = 1024
PAIR = 2

epsilon = 1e-06
loss_scale = 64.0


f32, bf16 = jnp.float32, jnp.bfloat16


def dot(left, right, contract):
    return lax.dot_general(left, right, (contract, ((), ())), preferred_element_type=f32)


def silu_slope(logits):
    sigmoid = jax.nn.sigmoid(logits)
    return sigmoid * (1.0 + logits * (1.0 - sigmoid))


def pick(stacked, index):
    return lax.dynamic_index_in_dim(stacked, index, 0, keepdims=False)


def after(value, *earlier):
    return lax.optimization_barrier((value, *earlier))[0]


def expand(weights, value):
    units, width = weights.shape
    steps = max(n for n in (4, 2, 1) if units % (16 * n) == 0 or n == 1)
    size = units // steps

    def kernel(weights_ref, value_ref, out_ref, held, done):
        def fetch(i):
            at = pl.ds(pl.multiple_of(i * size, size), size)
            return at, pltpu.make_async_copy(weights_ref.at[at], held.at[at], done.at[i])

        for i in range(steps):
            fetch(i)[1].start()

        def step(i, carry):
            at, copy = fetch(i)
            copy.wait()
            out_ref[at, :] = jax.nn.silu(dot(held[at, :], value_ref[...], ((1,), (0,)))).astype(bf16)
            return carry

        lax.fori_loop(0, steps, step, 0)

    vmem = pl.BlockSpec(memory_space=pltpu.VMEM)
    return pl.pallas_call(
        kernel,
        out_shape=jax.ShapeDtypeStruct((units, value.shape[1]), bf16),
        in_specs=[pl.BlockSpec(memory_space=pl.ANY), vmem],
        out_specs=vmem,
        scratch_shapes=[pltpu.VMEM((units, width), bf16), pltpu.SemaphoreType.DMA((steps,))],
        compiler_params=pltpu.CompilerParams(vmem_limit_bytes=2 * units * width + 20 * 2**20),
        cost_estimate=pl.CostEstimate(
            flops=2 * units * width * value.shape[1],
            transcendentals=units * value.shape[1],
            bytes_accessed=2 * (units * width + (units + width) * value.shape[1]),
        ),
    )(weights, value)


def tiles(own, other, values, flags, spare):
    piece, rows = own.shape[0], values[0][0].shape[1]
    half = rows // 2

    def kernel(flags_ref, own_ref, other_ref, *refs):
        kept_ref, given_ref = refs[-2:]
        first, low = flags_ref[0] == 0, flags_ref[1] == 0
        at = 0
        for i, value in enumerate(values):
            held = refs[at][...]
            if len(value) == 2:
                held = jnp.where(flags_ref[2] == 1, held, refs[at + 1][...])
            at += len(value)
            mine = dot(own_ref[...], held, ((1,), (0,)))
            theirs = dot(other_ref[...], held, ((1,), (0,)))
            blank = jnp.zeros((spare, rows), f32)
            top = jnp.concatenate([jnp.where(first, mine, theirs), blank], axis=0)
            bottom = jnp.concatenate([blank, jnp.where(first, theirs, mine)], axis=0)
            for j, part in enumerate((top, bottom)):
                left, right = part[:, :half].astype(bf16), part[:, half:].astype(bf16)
                kept_ref[i, j] = jnp.where(low, left, right)
                given_ref[i, j] = jnp.where(low, right, left)

    vmem = pl.BlockSpec(memory_space=pltpu.VMEM)
    shape = jax.ShapeDtypeStruct((len(values), 2, piece + spare, half), bf16)
    arrays = [array for value in values for array in value]
    return pl.pallas_call(
        kernel,
        out_shape=(shape, shape),
        in_specs=[pl.BlockSpec(memory_space=pltpu.SMEM)] + [vmem] * (2 + len(arrays)),
        out_specs=(vmem, vmem),
        compiler_params=pltpu.CompilerParams(vmem_limit_bytes=12 * 2**20),
    )(flags, own, other, *arrays)


def window_grads(late, early, units, side, line, block, window):
    offset = block - window
    own = units.shape[0] // 2

    def kernel(side_ref, late_ref, early_ref, units_ref, kept_ref, given_ref, theirs_ref):
        first = side_ref[0] == 0
        for z in range(line):
            halves = []
            for start in (z * block, z * block + offset):
                rows = pl.ds(start, window)
                features = jnp.concatenate([late_ref[rows, :], early_ref[rows, :]], axis=1)
                halves.append(dot(units_ref[...], features, ((1,), (1,))))
            low, high = halves
            kept, given = jnp.where(first, low, high), jnp.where(first, high, low)
            kept_ref[z] = kept[:own]
            given_ref[z] = given[:own]
            theirs_ref[0, z] = kept[own:].astype(bf16)
            theirs_ref[1, z] = given[own:].astype(bf16)

    shape = (line, own, window)
    vmem = pl.BlockSpec(memory_space=pltpu.VMEM)
    return pl.pallas_call(
        kernel,
        out_shape=(
            jax.ShapeDtypeStruct(shape, f32),
            jax.ShapeDtypeStruct(shape, f32),
            jax.ShapeDtypeStruct((2, *shape), bf16),
        ),
        in_specs=[pl.BlockSpec(memory_space=pltpu.SMEM), vmem, vmem, vmem],
        out_specs=(vmem, vmem, vmem),
        compiler_params=pltpu.CompilerParams(vmem_limit_bytes=8 * late.size + 2**23),
    )(side.reshape(1), late, early, units)


def body(
    teacher_state,
    injection,
    teacher_up,
    teacher_down,
    student_up,
    student_down,
    teacher_step,
    student_depth,
):
    slices, groups = lax.axis_size("tp"), lax.axis_size("grp")
    line = groups // PAIR
    member, group = lax.axis_index("tp"), lax.axis_index("grp")
    spot, side = group // PAIR, group % PAIR
    core, row = member % 2, member // 2
    rows, width = teacher_state.shape
    half = rows // 2
    units, piece = student_down.shape
    block = PAIR * piece
    window = (piece + 7) // 8 * 8
    offset = block - window

    def swap_side(value):
        return lax.ppermute(value, "grp", [(g, g ^ 1) for g in range(groups)])

    def send(value, moves):
        pairs = [(a * PAIR + s, b * PAIR + s) for a, b in moves for s in range(PAIR)]
        return lax.ppermute(value, "grp", pairs)

    def along(value, hop):
        return send(value, [(z, z ^ hop) for z in range(line)])

    def swap_core(value):
        return lax.ppermute(value, "tp", [(t, t ^ 1) for t in range(slices)])

    def swap_y(value):
        return lax.ppermute(value, "tp", [(t, t ^ 2) for t in range(slices)])

    down_own = teacher_down.T
    down_other = swap_side(down_own)
    small = jnp.concatenate([student_up, student_down.T], axis=1)
    spare = window - piece
    small = jnp.where(
        side == 0,
        jnp.pad(small, ((0, spare), (0, 0))),
        jnp.pad(small, ((spare, 0), (0, 0))),
    )
    arrived = [along(small, hop) for hop in range(1, line)]

    state = teacher_state.T
    inject = injection.T
    summed = state.astype(f32) + inject.astype(f32)
    factor = lax.rsqrt(jnp.mean(summed * summed, axis=0, keepdims=True) + epsilon)
    normed = (summed * factor).astype(bf16)

    up_own = teacher_up.T
    if line == 4:
        share = width // slices
        quarter = lax.dynamic_slice_in_dim(normed, member * share, share, 0)
        far = send(quarter, [(0, 3), (3, 0)])
        own_block = expand(up_own, normed)
        middle = [(1, 2), (2, 1)]
        outward = [(1, 0), (2, 3)]
        inner = (spot == 1) | (spot == 2)
        near = along(own_block, 1)
        cross_own = send(own_block, middle)
        other = swap_y(far)
        far = jnp.stack([far, swap_core(far), other, swap_core(other)])
        far = jnp.concatenate([pick(far, member ^ t) for t in range(slices)], axis=0)
        far = lax.optimization_barrier(far)
        far_block = expand(up_own, far)
        out_own = send(cross_own, outward)
        cross_next = send(near, middle)
        blocks = [
            (own_block,),
            (near,),
            (cross_next, out_own),
            (cross_own, far_block),
        ]
    else:
        own_block = expand(up_own, normed)
        inner = spot < 0
        blocks = [(own_block,)]
        blocks += [(along(own_block, hop),) for hop in range(1, line)]

    arrived = jnp.stack([small] + arrived)
    arrived = jnp.stack([pick(arrived, spot ^ z) for z in range(line)])
    arrived = after(arrived, own_block)
    other = swap_y(arrived)
    parts = jnp.stack(
        [
            jnp.concatenate([arrived[:, :, :units], other[:, :, :units]], axis=2),
            jnp.concatenate([arrived[:, :, units:], other[:, :, units:]], axis=2),
        ]
    )
    other = swap_side(parts)
    first, second = jnp.where(side == 0, parts, other), jnp.where(side == 0, other, parts)
    tail = ((0, 0), (0, 0), (0, offset), (0, 0))
    head = ((0, 0), (0, 0), (offset, 0), (0, 0))
    parts = (jnp.pad(first, tail) + jnp.pad(second, head)).reshape(2, width, 2 * units)
    other = swap_core(parts)
    up_all, down_all = lax.optimization_barrier(
        tuple(jnp.concatenate([parts[i], other[i]], axis=1) for i in range(2))
    )

    flags = jnp.stack([side, core, inner.astype(jnp.int32)])

    def both(first, second, axis):
        return jnp.where(
            row == 0, jnp.stack([first, second], axis=axis), jnp.stack([second, first], axis=axis)
        )

    deltas = [None] * line
    order = [[0, 1], [3, 2]] if line == 4 else [[hop] for hop in range(line)]
    for hops in order:
        values = [blocks[hop] for hop in hops]
        kept, given = tiles(down_own, down_other, values, flags, window - piece)
        other = swap_core(given)
        chip = (kept.astype(f32) + other.astype(f32)).astype(bf16)
        mine = lax.dynamic_index_in_dim(chip, row, 1, keepdims=False)
        theirs = lax.dynamic_index_in_dim(chip, 1 - row, 1, keepdims=False)
        other = swap_y(theirs)
        part = (mine.astype(f32) + other.astype(f32)).astype(bf16)
        pieces = [part[i] for i in range(len(hops))]
        part = jnp.stack([along(piece, hop) if hop else piece for piece, hop in zip(pieces, hops)])
        features = both(part, swap_y(part), 1)
        tail, head = ((0, 0), (0, offset), (0, 0)), ((0, 0), (offset, 0), (0, 0))
        features = jnp.pad(features[:, 0], tail) + jnp.pad(features[:, 1], head)
        for i, hop in enumerate(hops):
            deltas[hop] = features[i]
    deltas = jnp.stack(deltas)
    delta = jnp.stack([pick(deltas, spot ^ z) for z in range(line)])
    delta = delta.reshape(width, half)

    whole = lax.optimization_barrier((state, inject, normed, own_block))[:3]
    state, inject, normed1 = lax.optimization_barrier(
        tuple(jnp.where(core == 0, value[:, :half], value[:, half:]) for value in whole)
    )
    logits1 = dot(up_all, normed1, ((0,), (0,)))
    hidden1 = jax.nn.silu(logits1).astype(bf16)
    state1 = (state.astype(f32) + dot(down_all, hidden1, ((1,), (0,)))).astype(bf16)
    summed2 = state1.astype(f32) + inject.astype(f32)
    factor2 = lax.rsqrt(jnp.sum(summed2 * summed2, axis=0, keepdims=True) / width + epsilon)
    normed2 = (summed2 * factor2).astype(bf16)
    logits2 = dot(up_all, normed2, ((0,), (0,)))
    hidden2 = jax.nn.silu(logits2).astype(bf16)
    state2 = (state1.astype(f32) + dot(down_all, hidden2, ((1,), (0,)))).astype(bf16)

    first = group * rows + core * half
    sequence = (first + jnp.arange(half, dtype=jnp.int32)) // LENGTH
    steps = jnp.arange(teacher_step.shape[0], dtype=jnp.int32)[:, None]
    matches = sequence[None, :] == steps
    pick_teacher = jnp.sum(jnp.where(matches, teacher_step[:, None], 0), axis=0)[None, :]
    pick_depth = jnp.sum(jnp.where(matches, student_depth[:, None], 0), axis=0)[None, :]
    result = jnp.where(pick_depth == 1, state1, state2)
    result, state, summed2, factor2, normed2, logits1, logits2, hidden1, hidden2 = (
        lax.optimization_barrier(
            (result, state, summed2, factor2, normed2, logits1, logits2, hidden1, hidden2)
        )
    )

    def chip_units(value):
        return jnp.concatenate([value[:units], value[2 * units : 3 * units]], axis=0)

    def paired(late, early, units_late, units_early):
        joined = jnp.concatenate([chip_units(units_late), chip_units(units_early)], axis=1)
        kept, given, theirs = window_grads(late, early, joined, side, line, block, window)
        theirs = swap_core(theirs).astype(f32)
        other = swap_side((given + theirs[1]).astype(bf16))
        return (kept + theirs[0] + other.astype(f32)).astype(bf16)

    def lined(value):
        total = pick(value, spot).astype(f32)
        for hop in range(1, line):
            moved = along(pick(value, spot ^ hop), hop)
            total = total + moved.astype(f32)
        return jnp.where(side == 0, total[:, :piece], total[:, window - piece :])

    latent = (state.astype(f32) + delta.astype(f32)).astype(bf16)
    target = jnp.where(pick_teacher == 1, latent, state).astype(f32)
    slope = loss_scale * 2.0 / (rows * groups) * (result.astype(f32) - target)
    cotangent2 = jnp.where(pick_depth == 2, slope, 0.0)
    rounded2 = cotangent2.astype(bf16)
    upstream2 = dot(down_all, rounded2, ((0,), (0,)))
    local2 = (upstream2 * silu_slope(logits2)).astype(bf16)
    back_flow = dot(up_all, local2, ((1,), (0,)))
    mean_flow = jnp.sum(summed2 * back_flow, axis=0, keepdims=True) / width
    cotangent1 = (
        cotangent2
        + factor2 * back_flow
        - summed2 * factor2**3 * mean_flow
        + jnp.where(pick_depth == 1, slope, 0.0)
    )
    rounded1 = cotangent1.astype(bf16)
    grad_down = paired(rounded2, rounded1, hidden2, hidden1)
    upstream1 = dot(down_all, rounded1, ((0,), (0,)))
    local1 = (upstream1 * silu_slope(logits1)).astype(bf16)
    grad_up = paired(normed2, normed1, local2, local1)
    return lined(grad_up).T, lined(grad_down)


def solution(mesh):
    in_specs = (
        P("grp", None),
        P("grp", None),
        P(None, "tp"),
        P("tp", "grp"),
        P("grp", "tp"),
        P("tp", "grp"),
        P(),
        P(),
    )
    out_specs = (P("grp", "tp"), P("tp", "grp"))

    return jax.shard_map(body, mesh=mesh, in_specs=in_specs, out_specs=out_specs, check_vma=False)
```
